128 devices in a mesh: row: 4 (over x), col: 32 (over z, y, core).
Axes of the slice: x: 4, y: 4, z: 4, core: 2. Of those that a mesh axis runs over, the one named last changes fastest.
Arguments:
- amplitudes: float32 [1024, 16384], P(None, ('row', 'col')), may hold values from -6 to 6
- integrals: float32 [16384, 16384], P('row', 'col'), may hold values from -0.078125 to 0.078125
- vv_coupling: float32 [128, 128], replicated, may hold values from -0.5 to 0.5
- amp_mask: int32 [32, 128], replicated, may hold values 0 or 1
- integral_mask: int32 [128, 128], replicated, may hold values from 0 to 1, as said below
Outputs:
- residual: float32 [32, 32, 128, 128], P('row', 'col')
The draws below stay inside these ranges and needn't reach their ends.
Inputs may be any that keep to these rules, and one draw needn't show every extreme that they name: `amp_mask`: 1 keeps the amplitude tile (i, c), 0 screens it out. `integral_mask`: 1 keeps the integral tile (c, a), 0 screens it out.
All inputs are finite; a program needn't handle non-finite values.
Results may differ from the reference program's by a relative error of at most 0.00007.
Values sent between devices are 32-bit elements; how exact they have to be, the bound alone decides.
A program may use at most 192 MiB of HBM per device.

```python
import jax
import jax.numpy as jnp
from jax import lax

NV = 128
NJ = 32
NI = 32
PAIRS = 1024
VPAIRS = 16384


def draw_integral_mask(key, part):
    tiles = jnp.arange(NV, dtype=jnp.int32)
    limit = 100 + 800 * tiles // NV
    coins = jax.random.randint(key, (NV, NV), 0, 1000, dtype=jnp.int32)
    return (coins < limit[:, None]).astype(jnp.int32)


def plant(result, rng, least, largest):
    shape = result.shape
    place = [jax.random.randint(jax.random.fold_in(rng, axis), (), 0, shape[axis]) for axis in range(len(shape))]
    result = result.at[tuple(place)].set(least)
    longest = shape.index(max(shape))
    place[longest] = (place[longest] + 1) % shape[longest]
    return result.at[tuple(place)].set(largest)


def levels(stream_key, shape, pieces, smallest, largest):
    def one(dim, shards_of):
        draws = jax.random.uniform(jax.random.fold_in(jax.random.fold_in(stream_key, 6), dim), (shards_of,), jnp.float32, smallest / len(pieces), largest / len(pieces))
        return jnp.repeat(jnp.exp(draws), shape[dim] // shards_of).reshape((-1,) + (1,) * (len(shape) - dim - 1))

    gain = one(*pieces[0])
    for cut in pieces[1:]:
        gain = gain * one(*cut)
    return gain


def scatter_about(own_key, dims, deviation, bound, cuts=(), kind=jnp.bfloat16):
    values = jax.random.normal(own_key, dims, jnp.float32) * deviation
    if len(cuts) > 0:
        values = levels(own_key, dims, cuts, -0.22, 0.18) * values
    return jnp.clip(values, min=-bound, max=bound).astype(kind)


def setup_inputs(seed: int = 0) -> dict:
    key_list = jax.random.split(jax.random.key(seed), 6)
    return {
        "amplitudes": scatter_about(key_list[0], (PAIRS, VPAIRS), 1.0, 6.0, ((1, 128),), jnp.float32),
        "integrals": scatter_about(key_list[1], (VPAIRS, VPAIRS), (VPAIRS // 3) ** -0.5, 0.078125, ((0, 4), (1, 32)), jnp.float32),
        "vv_coupling": scatter_about(key_list[2], (NV, NV), NV ** -0.5, 0.5, (), jnp.float32),
        "amp_mask": plant((jax.random.randint(key_list[3], (NI, NV), 0, 3) < 2).astype(jnp.int32), jax.random.fold_in(key_list[3], 1), 0, 1),
        "integral_mask": draw_integral_mask(jax.random.fold_in(key_list[5], 71), 0),
    }


def reference(amplitudes, integrals, vv_coupling, amp_mask, integral_mask):
    amp_four = amplitudes.reshape(NI, NJ, NV, NV) * amp_mask.astype(jnp.float32)[:, None, :, None]
    int_four = integrals.reshape(NV, NV, NV, NV) * integral_mask.astype(jnp.float32)[:, None, :, None]
    ladder = jnp.dot(amp_four.reshape(PAIRS, VPAIRS), int_four.reshape(VPAIRS, VPAIRS), precision=lax.Precision.HIGHEST)
    blocks = ladder.reshape(NI, NJ, NV, NV)
    dressed = jnp.einsum("ac,ijcb->ijab", vv_coupling, blocks, precision=lax.Precision.HIGHEST)
    return blocks + dressed
```

```python
import jax
import jax.numpy as jnp
from jax import lax
from jax.sharding import Mesh
from jax.sharding import PartitionSpec as P

COL = ("zy", "core")


def body(amplitudes, integrals, vv_coupling, amp_mask, integral_mask):
    n_row = lax.axis_size("row")
    n_zy = lax.axis_size("zy")
    n_core = lax.axis_size("core")
    n_col = n_zy * n_core
    row_id = lax.axis_index("row")
    core_id = lax.axis_index("core")
    col_id = lax.axis_index("zy") * n_core + core_id
    virt = vv_coupling.shape[0]
    pairs, k_local = amplitudes.shape
    occ_i = amp_mask.shape[0]
    occ_j = pairs // occ_i

    c_own = row_id * n_col + col_id
    amp_col = lax.dynamic_slice_in_dim(amp_mask, c_own, 1, axis=1).astype(jnp.float32)
    amp_screened = (amplitudes.reshape(occ_i, occ_j, k_local) * amp_col[:, :, None]).reshape(
        pairs, k_local
    )

    c_rows = virt // n_row
    a_cols = virt // n_col
    n_local = a_cols * virt
    mask_local = lax.dynamic_slice(
        integral_mask, (row_id * c_rows, col_id * a_cols), (c_rows, a_cols)
    ).astype(jnp.float32)
    ints = integrals.reshape(n_zy, n_core, k_local, a_cols, virt) * mask_local.reshape(
        n_zy, n_core, 1, a_cols, 1
    )
    ints = ints.transpose(1, 0, 2, 3, 4).reshape(n_core, n_zy * k_local, n_local)

    own = lax.all_gather(amp_screened, "zy", axis=1, tiled=True)
    other = lax.ppermute(own, "core", [(0, 1), (1, 0)])
    ints_own = lax.dynamic_index_in_dim(ints, core_id, 0, keepdims=False)
    ints_other = lax.dynamic_index_in_dim(ints, 1 - core_id, 0, keepdims=False)
    partial = jnp.dot(own, ints_own, precision=lax.Precision.HIGHEST) + jnp.dot(
        other, ints_other, precision=lax.Precision.HIGHEST
    )

    ladder = lax.psum_scatter(partial, "row", scatter_dimension=0, tiled=True)
    i_local = pairs // n_row // occ_j
    blocks = ladder.reshape(i_local, occ_j, a_cols, virt)
    block = lax.all_to_all(blocks, COL, split_axis=1, concat_axis=2, tiled=True)
    return block + jnp.einsum("ac,ijcb->ijab", vv_coupling, block, precision=lax.Precision.HIGHEST)


def solution(mesh):
    n_row, n_col = mesh.devices.shape
    mesh3 = Mesh(mesh.devices.reshape(n_row, n_col // 2, 2), ("row",) + COL)
    in_specs = (P(None, ("row",) + COL), P("row", COL), P(), P(), P())
    out_specs = P("row", COL, None, None)
    return jax.shard_map(body, mesh=mesh3, in_specs=in_specs, out_specs=out_specs, check_vma=False)
```

```python
import jax
import jax.numpy as jnp
from jax import lax
from jax.sharding import Mesh
from jax.sharding import PartitionSpec as P

PLANE = ("z", "y")
COL = PLANE + ("core",)


def body(amplitudes, integrals, vv_coupling, amp_mask, integral_mask):
    n_row = lax.axis_size("row")
    n_zy = lax.axis_size(PLANE)
    n_core = lax.axis_size("core")
    n_col = n_zy * n_core
    row_id = lax.axis_index("row")
    core_id = lax.axis_index("core")
    col_id = lax.axis_index(PLANE) * n_core + core_id
    virt = vv_coupling.shape[0]
    pairs, k_local = amplitudes.shape
    occ_i = amp_mask.shape[0]
    occ_j = pairs // occ_i

    c_own = row_id * n_col + col_id
    amp_col = lax.dynamic_slice_in_dim(amp_mask, c_own, 1, axis=1).astype(jnp.float32)
    amp_screened = (amplitudes.reshape(occ_i, occ_j, k_local) * amp_col[:, :, None]).reshape(
        pairs, k_local
    )

    c_rows = virt // n_row
    a_cols = virt // n_col
    n_local = a_cols * virt
    mask_local = lax.dynamic_slice(
        integral_mask, (row_id * c_rows, col_id * a_cols), (c_rows, a_cols)
    ).astype(jnp.float32)
    mask_wide = jnp.repeat(mask_local, virt, axis=1)
    ints = integrals.reshape(n_zy, n_core, k_local, n_local) * mask_wide.reshape(
        n_zy, n_core, 1, n_local
    )

    own = lax.all_gather(amp_screened, PLANE, axis=1, tiled=True)
    other = lax.ppermute(own, "core", [(0, 1), (1, 0)])
    ints_own = lax.dynamic_index_in_dim(ints, core_id, 1, keepdims=False)
    ints_other = lax.dynamic_index_in_dim(ints, 1 - core_id, 1, keepdims=False)
    own = own.reshape(pairs, n_zy, k_local)
    other = other.reshape(pairs, n_zy, k_local)
    dims = (((1, 2), (0, 1)), ((), ()))
    partial = lax.dot_general(own, ints_own, dims, precision=lax.Precision.HIGH) + lax.dot_general(
        other, ints_other, dims, precision=lax.Precision.HIGH
    )

    ladder = lax.psum_scatter(partial, "row", scatter_dimension=0, tiled=True)
    i_local = pairs // n_row // occ_j
    blocks = ladder.reshape(i_local, occ_j, a_cols, virt)
    block = lax.all_to_all(blocks, COL, split_axis=1, concat_axis=2, tiled=True)
    return block + jnp.einsum("ac,ijcb->ijab", vv_coupling, block, precision=lax.Precision.HIGHEST)


def solution(mesh):
    n_row, n_col = mesh.devices.shape
    n_side = int(round((n_col // 2) ** 0.5))
    mesh3 = Mesh(mesh.devices.reshape(n_row, n_side, n_col // 2 // n_side, 2), ("row",) + COL)
    in_specs = (P(None, ("row",) + COL), P("row", COL), P(), P(), P())
    out_specs = P("row", COL, None, None)
    return jax.shard_map(body, mesh=mesh3, in_specs=in_specs, out_specs=out_specs, check_vma=False)
```

```python
import jax
import jax.numpy as jnp
from jax import lax
from jax.sharding import Mesh
from jax.sharding import PartitionSpec as P

PLANE = ("z", "y")
COL = PLANE + ("core",)
N_CHUNKS = 2


def shift(x, axis, step):
    n = lax.axis_size(axis)
    return lax.ppermute(x, axis, [(p, (p + step) % n) for p in range(n)])


def ring_gather(block, axis):
    n = lax.axis_size(axis)
    ahead = [block]
    behind = []
    for _ in range((n - 1) // 2):
        ahead.append(shift(ahead[-1], axis, -1))
        behind.append(shift(behind[-1] if behind else block, axis, +1))
    if n % 2 == 0 and n > 1:
        half = block.shape[0] // 2
        src_a = ahead[-1]
        src_b = behind[-1] if behind else block
        far = jnp.concatenate([shift(src_a[:half], axis, -1), shift(src_b[half:], axis, +1)], 0)
        ahead.append(far)
    return jnp.concatenate(ahead + behind[::-1], axis=1)


def body(amplitudes, integrals, vv_coupling, amp_mask, integral_mask):
    n_row = lax.axis_size("row")
    n_z = lax.axis_size("z")
    n_y = lax.axis_size("y")
    n_core = lax.axis_size("core")
    n_col = n_z * n_y * n_core
    row_id = lax.axis_index("row")
    z_id = lax.axis_index("z")
    y_id = lax.axis_index("y")
    core_id = lax.axis_index("core")
    col_id = (z_id * n_y + y_id) * n_core + core_id
    virt = vv_coupling.shape[0]
    pairs, k_local = amplitudes.shape
    occ_i = amp_mask.shape[0]
    occ_j = pairs // occ_i

    c_own = row_id * n_col + col_id
    amp_col = lax.dynamic_slice_in_dim(amp_mask, c_own, 1, axis=1).astype(jnp.float32)
    amp_screened = (amplitudes.reshape(occ_i, occ_j, k_local) * amp_col[:, :, None]).reshape(
        pairs, k_local
    )

    c_rows = virt // n_row
    a_cols = virt // n_col
    n_local = a_cols * virt
    mask_local = lax.dynamic_slice(
        integral_mask, (row_id * c_rows, col_id * a_cols), (c_rows, a_cols)
    ).astype(jnp.float32)
    mask_wide = jnp.repeat(mask_local, virt, axis=1)
    ints = integrals.reshape(c_rows, k_local, n_local) * mask_wide[:, None, :]
    dc = jnp.arange(n_core, dtype=jnp.int32)[:, None, None]
    dz = jnp.arange(n_z, dtype=jnp.int32)[None, :, None]
    dy = jnp.arange(n_y, dtype=jnp.int32)[None, None, :]
    tile = (((z_id + dz) % n_z) * n_y + (y_id + dy) % n_y) * n_core + (core_id + dc) % n_core
    ints_rel = jnp.take(ints, tile.reshape(-1), axis=0).reshape(n_core, n_z * n_y * k_local, n_local)

    i_local = occ_i // n_row
    i_chunk = i_local // N_CHUNKS
    amp_chunks = amp_screened.reshape(n_row, N_CHUNKS, i_chunk * occ_j, k_local)
    outs = []
    for h in range(N_CHUNKS):
        a_h = amp_chunks[:, h].reshape(n_row * i_chunk * occ_j, k_local)
        own = ring_gather(ring_gather(a_h, "y"), "z")
        other = lax.ppermute(own, "core", [(0, 1), (1, 0)])
        partial = jnp.dot(own, ints_rel[0], precision=lax.Precision.HIGH) + jnp.dot(
            other, ints_rel[1], precision=lax.Precision.HIGH
        )
        ladder = lax.psum_scatter(partial, "row", scatter_dimension=0, tiled=True)
        blocks = ladder.reshape(i_chunk, occ_j, a_cols, virt)
        outs.append(lax.all_to_all(blocks, COL, split_axis=1, concat_axis=2, tiled=True))
    block = jnp.concatenate(outs, axis=0)
    return block + jnp.einsum("ac,ijcb->ijab", vv_coupling, block, precision=lax.Precision.HIGHEST)


def solution(mesh):
    n_row, n_col = mesh.devices.shape
    n_side = int(round((n_col // 2) ** 0.5))
    mesh4 = Mesh(mesh.devices.reshape(n_row, n_side, n_col // 2 // n_side, 2), ("row",) + COL)
    in_specs = (P(None, ("row",) + COL), P("row", COL), P(), P(), P())
    out_specs = P("row", COL, None, None)
    return jax.shard_map(body, mesh=mesh4, in_specs=in_specs, out_specs=out_specs, check_vma=False)
```

```python
import jax
import jax.numpy as jnp
from jax import lax
from jax.sharding import Mesh
from jax.sharding import PartitionSpec as P

PLANE = ("z", "y")
COL = PLANE + ("core",)


def body(amplitudes, integrals, vv_coupling, amp_mask, integral_mask):
    n_row = lax.axis_size("row")
    n_zy = lax.axis_size(PLANE)
    n_core = lax.axis_size("core")
    n_col = n_zy * n_core
    row_id = lax.axis_index("row")
    core_id = lax.axis_index("core")
    col_id = lax.axis_index(PLANE) * n_core + core_id
    virt = vv_coupling.shape[0]
    pairs, k_local = amplitudes.shape
    occ_i = amp_mask.shape[0]
    occ_j = pairs // occ_i

    c_own = row_id * n_col + col_id
    amp_col = lax.dynamic_slice_in_dim(amp_mask, c_own, 1, axis=1).astype(jnp.float32)
    amp_screened = (amplitudes.reshape(occ_i, occ_j, k_local) * amp_col[:, :, None]).reshape(
        pairs, k_local
    )

    c_rows = virt // n_row
    a_cols = virt // n_col
    n_local = a_cols * virt
    mask_local = lax.dynamic_slice(
        integral_mask, (row_id * c_rows, col_id * a_cols), (c_rows, a_cols)
    ).astype(jnp.float32)
    mask_wide = jnp.repeat(mask_local, virt, axis=1)
    ints = integrals.reshape(n_zy, n_core, k_local, n_local)
    masks = mask_wide.reshape(n_zy, n_core, 1, n_local)
    ints_c0 = ints[:, 0] * masks[:, 0]
    ints_c1 = ints[:, 1] * masks[:, 1]

    own = lax.all_gather(amp_screened, PLANE, axis=1, tiled=True)
    other = lax.ppermute(own, "core", [(0, 1), (1, 0)])
    first = core_id == 0
    ints_own = jnp.where(first, ints_c0, ints_c1)
    ints_other = jnp.where(first, ints_c1, ints_c0)
    own = own.reshape(pairs, n_zy, k_local)
    other = other.reshape(pairs, n_zy, k_local)
    dims = (((1, 2), (0, 1)), ((), ()))
    partial = lax.dot_general(own, ints_own, dims, precision=lax.Precision.HIGH) + lax.dot_general(
        other, ints_other, dims, precision=lax.Precision.HIGH
    )

    ladder = lax.psum_scatter(partial, "row", scatter_dimension=0, tiled=True)
    i_local = pairs // n_row // occ_j
    blocks = ladder.reshape(i_local, occ_j, a_cols, virt)
    half = i_local // 2
    block = jnp.concatenate(
        [
            lax.all_to_all(blocks[:half], COL, split_axis=1, concat_axis=2, tiled=True),
            lax.all_to_all(blocks[half:], COL, split_axis=1, concat_axis=2, tiled=True),
        ],
        axis=0,
    )
    return block + jnp.einsum("ac,ijcb->ijab", vv_coupling, block, precision=lax.Precision.HIGHEST)


def solution(mesh):
    n_row, n_col = mesh.devices.shape
    n_side = int(round((n_col // 2) ** 0.5))
    mesh3 = Mesh(mesh.devices.reshape(n_row, n_side, n_col // 2 // n_side, 2), ("row",) + COL)
    in_specs = (P(None, ("row",) + COL), P("row", COL), P(), P(), P())
    out_specs = P("row", COL, None, None)
    return jax.shard_map(body, mesh=mesh3, in_specs=in_specs, out_specs=out_specs, check_vma=False)
```

```python
import jax
import jax.numpy as jnp
from jax import lax
from jax.sharding import Mesh
from jax.sharding import PartitionSpec as P

PLANE = ("z", "y")
COL = PLANE + ("core",)


def body(amplitudes, integrals, vv_coupling, amp_mask, integral_mask):
    n_row = lax.axis_size("row")
    n_zy = lax.axis_size(PLANE)
    n_core = lax.axis_size("core")
    n_col = n_zy * n_core
    row_id = lax.axis_index("row")
    core_id = lax.axis_index("core")
    col_id = lax.axis_index(PLANE) * n_core + core_id
    virt = vv_coupling.shape[0]
    pairs, k_local = amplitudes.shape
    occ_i = amp_mask.shape[0]
    occ_j = pairs // occ_i

    c_own = row_id * n_col + col_id
    amp_col = lax.dynamic_slice_in_dim(amp_mask, c_own, 1, axis=1).astype(jnp.float32)
    amp_screened = (amplitudes.reshape(occ_i, occ_j, k_local) * amp_col[:, :, None]).reshape(
        pairs, k_local
    )

    c_rows = virt // n_row
    a_cols = virt // n_col
    n_local = a_cols * virt
    mask_local = lax.dynamic_slice(
        integral_mask, (row_id * c_rows, col_id * a_cols), (c_rows, a_cols)
    ).astype(jnp.float32)
    mask_wide = jnp.repeat(mask_local, virt, axis=1)
    ints = integrals.reshape(n_zy, n_core, k_local, n_local)
    masks = mask_wide.reshape(n_zy, n_core, 1, n_local)
    ints_c0 = ints[:, 0] * masks[:, 0]
    ints_c1 = ints[:, 1] * masks[:, 1]

    own = lax.all_gather(amp_screened, PLANE, axis=1, tiled=True)
    other = lax.ppermute(own, "core", [(0, 1), (1, 0)])
    first = core_id == 0
    ints_own = jnp.where(first, ints_c0, ints_c1)
    ints_other = jnp.where(first, ints_c1, ints_c0)
    own = own.reshape(pairs, n_zy, k_local)
    other = other.reshape(pairs, n_zy, k_local)
    dims = (((1, 2), (0, 1)), ((), ()))
    partial = lax.dot_general(own, ints_own, dims, precision=lax.Precision.HIGH) + lax.dot_general(
        other, ints_other, dims, precision=lax.Precision.HIGH
    )

    pieces = lax.all_to_all(
        partial.reshape(n_row, pairs // n_row, n_local), "row", split_axis=0, concat_axis=0, tiled=True
    )
    ladder = pieces.sum(axis=0)
    i_local = pairs // n_row // occ_j
    blocks = ladder.reshape(i_local, occ_j, a_cols, virt)
    block = lax.all_to_all(blocks, COL, split_axis=1, concat_axis=2, tiled=True)
    return block + jnp.einsum("ac,ijcb->ijab", vv_coupling, block, precision=lax.Precision.HIGHEST)


def solution(mesh):
    n_row, n_col = mesh.devices.shape
    n_side = int(round((n_col // 2) ** 0.5))
    mesh3 = Mesh(mesh.devices.reshape(n_row, n_side, n_col // 2 // n_side, 2), ("row",) + COL)
    in_specs = (P(None, ("row",) + COL), P("row", COL), P(), P(), P())
    out_specs = P("row", COL, None, None)
    return jax.shard_map(body, mesh=mesh3, in_specs=in_specs, out_specs=out_specs, check_vma=False)
```

```python
import jax
import jax.numpy as jnp
from jax import lax
from jax.sharding import Mesh
from jax.sharding import PartitionSpec as P

PLANE = ("z", "y")
COL = PLANE + ("core",)


def body(amplitudes, integrals, vv_coupling, amp_mask, integral_mask):
    n_row = lax.axis_size("row")
    n_zy = lax.axis_size(PLANE)
    n_core = lax.axis_size("core")
    n_col = n_zy * n_core
    row_id = lax.axis_index("row")
    core_id = lax.axis_index("core")
    col_id = lax.axis_index(PLANE) * n_core + core_id
    virt = vv_coupling.shape[0]
    pairs, k_local = amplitudes.shape
    occ_i = amp_mask.shape[0]
    occ_j = pairs // occ_i

    amp_row = lax.dynamic_slice_in_dim(amp_mask, row_id * n_col, n_col, axis=1).astype(jnp.float32)
    amp_row = amp_row.reshape(occ_i, n_zy, n_core)

    c_rows = virt // n_row
    a_cols = virt // n_col
    n_local = a_cols * virt
    mask_local = lax.dynamic_slice(
        integral_mask, (row_id * c_rows, col_id * a_cols), (c_rows, a_cols)
    ).astype(jnp.float32)
    mask_wide = jnp.repeat(mask_local, virt, axis=1)
    ints = integrals.reshape(n_zy, n_core, k_local, n_local)
    masks = mask_wide.reshape(n_zy, n_core, 1, n_local)
    ints_c0 = ints[:, 0] * masks[:, 0]
    ints_c1 = ints[:, 1] * masks[:, 1]

    own = lax.all_gather(amplitudes, PLANE, axis=1, tiled=True)
    other = lax.ppermute(own, "core", [(0, 1), (1, 0)])
    first = core_id == 0
    ints_own = jnp.where(first, ints_c0, ints_c1)
    ints_other = jnp.where(first, ints_c1, ints_c0)
    amp_own = jnp.where(first, amp_row[:, :, 0], amp_row[:, :, 1])
    amp_other = jnp.where(first, amp_row[:, :, 1], amp_row[:, :, 0])
    own = (own.reshape(occ_i, occ_j, n_zy, k_local) * amp_own[:, None, :, None]).reshape(
        pairs, n_zy, k_local
    )
    other = (other.reshape(occ_i, occ_j, n_zy, k_local) * amp_other[:, None, :, None]).reshape(
        pairs, n_zy, k_local
    )
    dims = (((1, 2), (0, 1)), ((), ()))
    partial = lax.dot_general(own, ints_own, dims, precision=lax.Precision.HIGH) + lax.dot_general(
        other, ints_other, dims, precision=lax.Precision.HIGH
    )

    pieces = lax.all_to_all(
        partial.reshape(n_row, pairs // n_row, n_local), "row", split_axis=0, concat_axis=0, tiled=True
    )
    ladder = pieces.sum(axis=0)
    i_local = pairs // n_row // occ_j
    blocks = ladder.reshape(i_local, occ_j, a_cols, virt)
    block = lax.all_to_all(blocks, COL, split_axis=1, concat_axis=2, tiled=True)
    return block + jnp.einsum("ac,ijcb->ijab", vv_coupling, block, precision=lax.Precision.HIGHEST)


def solution(mesh):
    n_row, n_col = mesh.devices.shape
    n_side = int(round((n_col // 2) ** 0.5))
    mesh3 = Mesh(mesh.devices.reshape(n_row, n_side, n_col // 2 // n_side, 2), ("row",) + COL)
    in_specs = (P(None, ("row",) + COL), P("row", COL), P(), P(), P())
    out_specs = P("row", COL, None, None)
    return jax.shard_map(body, mesh=mesh3, in_specs=in_specs, out_specs=out_specs, check_vma=False)
```

```python
import jax
import jax.numpy as jnp
from jax import lax
from jax.sharding import Mesh
from jax.sharding import PartitionSpec as P

PLANE = ("z", "y")
COL = PLANE + ("core",)


def body(amplitudes, integrals, vv_coupling, amp_mask, integral_mask):
    n_row = lax.axis_size("row")
    n_zy = lax.axis_size(PLANE)
    n_core = lax.axis_size("core")
    n_col = n_zy * n_core
    row_id = lax.axis_index("row")
    core_id = lax.axis_index("core")
    col_id = lax.axis_index(PLANE) * n_core + core_id
    virt = vv_coupling.shape[0]
    pairs, k_local = amplitudes.shape
    occ_i = amp_mask.shape[0]
    occ_j = pairs // occ_i

    c_own = row_id * n_col + col_id
    amp_col = lax.dynamic_slice_in_dim(amp_mask, c_own, 1, axis=1).astype(jnp.float32)
    amp_screened = (amplitudes.reshape(occ_i, occ_j, k_local) * amp_col[:, :, None]).reshape(
        pairs, k_local
    )

    c_rows = virt // n_row
    a_cols = virt // n_col
    n_local = a_cols * virt
    mask_local = lax.dynamic_slice(
        integral_mask, (row_id * c_rows, col_id * a_cols), (c_rows, a_cols)
    ).astype(jnp.float32)
    mask_wide = jnp.repeat(mask_local, virt, axis=1)
    ints = integrals.reshape(n_zy, n_core, k_local, n_local)
    masks = mask_wide.reshape(n_zy, n_core, 1, n_local)
    ints_c0 = ints[:, 0] * masks[:, 0]
    ints_c1 = ints[:, 1] * masks[:, 1]

    own = lax.all_gather(amp_screened, PLANE, axis=1, tiled=True)
    other = lax.ppermute(own, "core", [(0, 1), (1, 0)])
    first = core_id == 0
    ints_own = jnp.where(first, ints_c0, ints_c1)
    ints_other = jnp.where(first, ints_c1, ints_c0)
    own = own.reshape(pairs, n_zy, k_local)
    other = other.reshape(pairs, n_zy, k_local)
    dims = (((1, 2), (0, 1)), ((), ()))
    partial = lax.dot_general(own, ints_own, dims, precision=lax.Precision.HIGH) + lax.dot_general(
        other, ints_other, dims, precision=lax.Precision.HIGH
    )

    i_local = pairs // n_row // occ_j
    buf = partial.reshape(n_row, i_local, occ_j, a_cols, virt).transpose(0, 2, 1, 3, 4)
    buf = buf.reshape(n_row * occ_j, i_local, a_cols, virt)
    recv = lax.all_to_all(buf, ("row",) + COL, split_axis=0, concat_axis=0, tiled=True)
    summed = recv.reshape(n_row, n_col, i_local, a_cols, virt).sum(axis=0)
    block = summed.transpose(1, 0, 2, 3).reshape(i_local, 1, n_col * a_cols, virt)
    return block + jnp.einsum("ac,ijcb->ijab", vv_coupling, block, precision=lax.Precision.HIGHEST)


def solution(mesh):
    n_row, n_col = mesh.devices.shape
    n_side = int(round((n_col // 2) ** 0.5))
    mesh3 = Mesh(mesh.devices.reshape(n_row, n_side, n_col // 2 // n_side, 2), ("row",) + COL)
    in_specs = (P(None, ("row",) + COL), P("row", COL), P(), P(), P())
    out_specs = P("row", COL, None, None)
    return jax.shard_map(body, mesh=mesh3, in_specs=in_specs, out_specs=out_specs, check_vma=False)
```

```python
import jax
import jax.numpy as jnp
from jax import lax
from jax.sharding import Mesh
from jax.sharding import PartitionSpec as P

PLANE = ("z", "y")
COL = PLANE + ("core",)


def body(amplitudes, integrals, vv_coupling, amp_mask, integral_mask):
    n_row = lax.axis_size("row")
    n_zy = lax.axis_size(PLANE)
    n_core = lax.axis_size("core")
    n_col = n_zy * n_core
    row_id = lax.axis_index("row")
    core_id = lax.axis_index("core")
    col_id = lax.axis_index(PLANE) * n_core + core_id
    virt = vv_coupling.shape[0]
    pairs, k_local = amplitudes.shape
    occ_i = amp_mask.shape[0]
    occ_j = pairs // occ_i

    c_own = row_id * n_col + col_id
    amp_col = lax.dynamic_slice_in_dim(amp_mask, c_own, 1, axis=1).astype(jnp.float32)
    amp_screened = (amplitudes.reshape(occ_i, occ_j, k_local) * amp_col[:, :, None]).reshape(
        pairs, k_local
    )

    c_rows = virt // n_row
    a_cols = virt // n_col
    n_local = a_cols * virt
    mask_local = lax.dynamic_slice(
        integral_mask, (row_id * c_rows, col_id * a_cols), (c_rows, a_cols)
    ).astype(jnp.float32)
    mask_wide = jnp.repeat(mask_local, virt, axis=1)
    ints = integrals.reshape(n_zy, n_core, k_local, n_local)
    masks = mask_wide.reshape(n_zy, n_core, 1, n_local)
    ints_c0 = ints[:, 0] * masks[:, 0]
    ints_c1 = ints[:, 1] * masks[:, 1]

    own = lax.all_gather(amp_screened, PLANE, axis=1, tiled=True)
    other = lax.ppermute(own, "core", [(0, 1), (1, 0)])
    first = core_id == 0
    ints_own = jnp.where(first, ints_c0, ints_c1)
    ints_other = jnp.where(first, ints_c1, ints_c0)
    own = own.reshape(pairs, n_zy, k_local)
    other = other.reshape(pairs, n_zy, k_local)
    dims = (((1, 2), (0, 1)), ((), ()))

    i_local = pairs // n_row // occ_j
    n_half = n_local // 2
    halves = []
    for h in range(2):
        cols = slice(h * n_half, (h + 1) * n_half)
        partial = lax.dot_general(
            own, ints_own[..., cols], dims, precision=lax.Precision.HIGH
        ) + lax.dot_general(other, ints_other[..., cols], dims, precision=lax.Precision.HIGH)
        buf = partial.reshape(n_row, i_local, occ_j, n_half).transpose(0, 2, 1, 3)
        buf = buf.reshape(n_row * occ_j, i_local, n_half)
        recv = lax.all_to_all(buf, ("row",) + COL, split_axis=0, concat_axis=0, tiled=True)
        halves.append(recv.reshape(n_row, n_col, i_local, n_half).sum(axis=0))
    summed = jnp.stack(halves, axis=2)
    block = summed.transpose(1, 0, 2, 3).reshape(i_local, 1, n_col * a_cols, virt)
    return block + jnp.einsum("ac,ijcb->ijab", vv_coupling, block, precision=lax.Precision.HIGHEST)


def solution(mesh):
    n_row, n_col = mesh.devices.shape
    n_side = int(round((n_col // 2) ** 0.5))
    mesh3 = Mesh(mesh.devices.reshape(n_row, n_side, n_col // 2 // n_side, 2), ("row",) + COL)
    in_specs = (P(None, ("row",) + COL), P("row", COL), P(), P(), P())
    out_specs = P("row", COL, None, None)
    return jax.shard_map(body, mesh=mesh3, in_specs=in_specs, out_specs=out_specs, check_vma=False)
```

```python
import jax
import jax.numpy as jnp
from jax import lax
from jax.sharding import Mesh
from jax.sharding import PartitionSpec as P

PLANE = ("z", "y")
COL = PLANE + ("core",)


def body(amplitudes, integrals, vv_coupling, amp_mask, integral_mask):
    n_row = lax.axis_size("row")
    n_zy = lax.axis_size(PLANE)
    n_core = lax.axis_size("core")
    n_col = n_zy * n_core
    row_id = lax.axis_index("row")
    core_id = lax.axis_index("core")
    col_id = lax.axis_index(PLANE) * n_core + core_id
    virt = vv_coupling.shape[0]
    pairs, k_local = amplitudes.shape
    occ_i = amp_mask.shape[0]
    occ_j = pairs // occ_i

    c_own = row_id * n_col + col_id
    amp_col = lax.dynamic_slice_in_dim(amp_mask, c_own, 1, axis=1).astype(jnp.float32)
    amp_screened = (amplitudes.reshape(occ_i, occ_j, k_local) * amp_col[:, :, None]).reshape(
        pairs, k_local
    )

    c_rows = virt // n_row
    a_cols = virt // n_col
    n_local = a_cols * virt
    mask_local = lax.dynamic_slice(
        integral_mask, (row_id * c_rows, col_id * a_cols), (c_rows, a_cols)
    ).astype(jnp.float32)
    mask_wide = jnp.repeat(mask_local, virt, axis=1)
    ints = integrals.reshape(n_zy, n_core, k_local, n_local)
    masks = mask_wide.reshape(n_zy, n_core, 1, n_local)
    ints_c0 = ints[:, 0] * masks[:, 0]
    ints_c1 = ints[:, 1] * masks[:, 1]

    own = lax.all_gather(amp_screened, PLANE, axis=1, tiled=True)
    other = lax.ppermute(own, "core", [(0, 1), (1, 0)])
    first = core_id == 0
    ints_own = jnp.where(first, ints_c0, ints_c1)
    ints_other = jnp.where(first, ints_c1, ints_c0)
    own = own.reshape(pairs, n_zy, k_local)
    other = other.reshape(pairs, n_zy, k_local)
    dims = (((1, 2), (0, 1)), ((), ()))
    partial = lax.dot_general(own, ints_own, dims, precision=lax.Precision.HIGH) + lax.dot_general(
        other, ints_other, dims, precision=lax.Precision.HIGH
    )

    i_local = pairs // n_row // occ_j
    buf = partial.reshape(n_row, i_local, occ_j, a_cols, virt).transpose(0, 2, 1, 3, 4)
    buf = buf.reshape(n_row * occ_j, i_local, a_cols, virt)
    recv = lax.all_to_all(buf, ("row",) + COL, split_axis=0, concat_axis=0, tiled=True)
    summed = recv.reshape(n_row, n_col, i_local, a_cols, virt).sum(axis=0)
    dressing = (jnp.eye(virt, dtype=vv_coupling.dtype) + vv_coupling).reshape(virt, n_col, a_cols)
    out = jnp.einsum("akc,kicb->iab", dressing, summed, precision=lax.Precision.HIGHEST)
    return out.reshape(i_local, 1, virt, virt)


def solution(mesh):
    n_row, n_col = mesh.devices.shape
    n_side = int(round((n_col // 2) ** 0.5))
    mesh3 = Mesh(mesh.devices.reshape(n_row, n_side, n_col // 2 // n_side, 2), ("row",) + COL)
    in_specs = (P(None, ("row",) + COL), P("row", COL), P(), P(), P())
    out_specs = P("row", COL, None, None)
    return jax.shard_map(body, mesh=mesh3, in_specs=in_specs, out_specs=out_specs, check_vma=False)
```

```python
import jax
import jax.numpy as jnp
from jax import lax
from jax.experimental.layout import Layout, with_layout_constraint
from jax.sharding import Mesh
from jax.sharding import PartitionSpec as P

PLANE = ("z", "y")
COL = PLANE + ("core",)


def body(amplitudes, integrals, vv_coupling, amp_mask, integral_mask):
    n_row = lax.axis_size("row")
    n_zy = lax.axis_size(PLANE)
    n_core = lax.axis_size("core")
    n_col = n_zy * n_core
    row_id = lax.axis_index("row")
    core_id = lax.axis_index("core")
    col_id = lax.axis_index(PLANE) * n_core + core_id
    virt = vv_coupling.shape[0]
    pairs, k_local = amplitudes.shape
    occ_i = amp_mask.shape[0]
    occ_j = pairs // occ_i

    c_own = row_id * n_col + col_id
    amp_col = lax.dynamic_slice_in_dim(amp_mask, c_own, 1, axis=1).astype(jnp.float32)
    i_local = occ_i // n_row
    amp_screened = amplitudes.reshape(occ_i, occ_j, k_local) * amp_col[:, :, None]
    amp_t = amp_screened.reshape(n_row, i_local, occ_j, k_local).transpose(3, 0, 2, 1)
    amp_t = with_layout_constraint(amp_t.reshape(k_local, pairs), Layout((0, 1)))

    c_rows = virt // n_row
    a_cols = virt // n_col
    n_local = a_cols * virt
    mask_local = lax.dynamic_slice(
        integral_mask, (row_id * c_rows, col_id * a_cols), (c_rows, a_cols)
    ).astype(jnp.float32)
    mask_wide = jnp.repeat(mask_local, virt, axis=1)
    ints = integrals.reshape(n_zy, n_core, k_local, n_local)
    masks = mask_wide.reshape(n_zy, n_core, 1, n_local)
    ints_c0 = ints[:, 0] * masks[:, 0]
    ints_c1 = ints[:, 1] * masks[:, 1]

    own = with_layout_constraint(lax.all_gather(amp_t, PLANE, axis=0, tiled=True), Layout((0, 1)))
    other = lax.ppermute(own, "core", [(0, 1), (1, 0)])
    first = core_id == 0
    ints_own = jnp.where(first, ints_c0, ints_c1)
    ints_other = jnp.where(first, ints_c1, ints_c0)
    own = own.reshape(n_zy, k_local, pairs)
    other = other.reshape(n_zy, k_local, pairs)
    dims = (((0, 1), (0, 1)), ((), ()))
    partial = lax.dot_general(own, ints_own, dims, precision=lax.Precision.HIGH) + lax.dot_general(
        other, ints_other, dims, precision=lax.Precision.HIGH
    )

    buf = partial.reshape(n_row * occ_j, i_local, a_cols, virt)
    recv = lax.all_to_all(buf, ("row",) + COL, split_axis=0, concat_axis=0, tiled=True)
    summed = recv.reshape(n_row, n_col, i_local, a_cols, virt).sum(axis=0)
    block = summed.transpose(1, 0, 2, 3).reshape(i_local, 1, n_col * a_cols, virt)
    return block + jnp.einsum("ac,ijcb->ijab", vv_coupling, block, precision=lax.Precision.HIGHEST)


def solution(mesh):
    n_row, n_col = mesh.devices.shape
    n_side = int(round((n_col // 2) ** 0.5))
    mesh3 = Mesh(mesh.devices.reshape(n_row, n_side, n_col // 2 // n_side, 2), ("row",) + COL)
    in_specs = (P(None, ("row",) + COL), P("row", COL), P(), P(), P())
    out_specs = P("row", COL, None, None)
    return jax.shard_map(body, mesh=mesh3, in_specs=in_specs, out_specs=out_specs, check_vma=False)
```

```python
import jax
import jax.numpy as jnp
from jax import lax
from jax.experimental.layout import Layout, with_layout_constraint
from jax.sharding import Mesh

from jax.sharding import PartitionSpec as P

PLANE = ("z", "y")
COL = PLANE + ("core",)


def body(amplitudes, integrals, vv_coupling, amp_mask, integral_mask):
    n_row = lax.axis_size("row")
    n_zy = lax.axis_size(PLANE)
    n_core = lax.axis_size("core")
    n_col = n_zy * n_core
    row_id = lax.axis_index("row")
    core_id = lax.axis_index("core")
    col_id = lax.axis_index(PLANE) * n_core + core_id
    virt = vv_coupling.shape[0]
    pairs, k_local = amplitudes.shape
    occ_i = amp_mask.shape[0]
    occ_j = pairs // occ_i

    c_own = row_id * n_col + col_id
    amp_col = lax.dynamic_slice_in_dim(amp_mask, c_own, 1, axis=1).astype(jnp.float32)
    i_local = occ_i // n_row
    amp_screened = amplitudes.reshape(occ_i, occ_j, k_local) * amp_col[:, :, None]
    amp_t = amp_screened.reshape(n_row, i_local, occ_j, k_local).transpose(3, 0, 2, 1)
    amp_t = with_layout_constraint(amp_t.reshape(k_local, pairs), Layout((0, 1)))

    c_rows = virt // n_row
    a_cols = virt // n_col
    n_local = a_cols * virt
    mask_local = lax.dynamic_slice(
        integral_mask, (row_id * c_rows, col_id * a_cols), (c_rows, a_cols)
    ).astype(jnp.float32)
    mask_wide = jnp.repeat(mask_local, virt, axis=1)
    ints = integrals.reshape(n_zy, n_core, k_local, n_local)
    masks = mask_wide.reshape(n_zy, n_core, 1, n_local)
    ints_c0 = ints[:, 0] * masks[:, 0]
    ints_c1 = ints[:, 1] * masks[:, 1]

    own = lax.all_gather(amp_t, PLANE, axis=0, tiled=True)
    own = with_layout_constraint(own, Layout((0, 1)))
    other = lax.ppermute(own, "core", [(0, 1), (1, 0)])
    first = core_id == 0
    ints_own = jnp.where(first, ints_c0, ints_c1)
    ints_other = jnp.where(first, ints_c1, ints_c0)
    ints_own, ints_other = lax.optimization_barrier((ints_own, ints_other))
    own = own.reshape(n_zy, k_local, pairs)
    other = other.reshape(n_zy, k_local, pairs)
    dims = (((0, 1), (0, 1)), ((), ()))
    partial = lax.dot_general(own, ints_own, dims, precision=lax.Precision.HIGH) + lax.dot_general(
        other, ints_other, dims, precision=lax.Precision.HIGH
    )

    buf = partial.reshape(n_row * occ_j, i_local, a_cols, virt)
    recv = lax.all_to_all(buf, ("row",) + COL, split_axis=0, concat_axis=0, tiled=True)
    summed = recv.reshape(n_row, n_col, i_local, a_cols, virt).sum(axis=0)
    block = summed.transpose(1, 0, 2, 3).reshape(i_local, 1, n_col * a_cols, virt)
    row_major = Layout((0, 1, 2, 3))
    block = with_layout_constraint(block, row_major)
    out = block + jnp.einsum("ac,ijcb->ijab", vv_coupling, block, precision=lax.Precision.HIGHEST)
    return with_layout_constraint(out, row_major)


def solution(mesh):
    n_row, n_col = mesh.devices.shape
    n_side = int(round((n_col // 2) ** 0.5))
    mesh3 = Mesh(mesh.devices.reshape(n_row, n_side, n_col // 2 // n_side, 2), ("row",) + COL)
    in_specs = (P(None, ("row",) + COL), P("row", COL), P(), P(), P())
    out_specs = P("row", COL, None, None)

    return jax.shard_map(body, mesh=mesh3, in_specs=in_specs, out_specs=out_specs, check_vma=False)
```

```python
import jax
import jax.numpy as jnp
from jax import lax
from jax.experimental.layout import Layout, with_layout_constraint
from jax.sharding import Mesh

from jax.sharding import PartitionSpec as P

PLANE = ("z", "y")
COL = PLANE + ("core",)


def body(amplitudes, integrals, vv_coupling, amp_mask, integral_mask):
    n_row = lax.axis_size("row")
    n_zy = lax.axis_size(PLANE)
    n_core = lax.axis_size("core")
    n_col = n_zy * n_core
    row_id = lax.axis_index("row")
    core_id = lax.axis_index("core")
    col_id = lax.axis_index(PLANE) * n_core + core_id
    virt = vv_coupling.shape[0]
    pairs, k_local = amplitudes.shape
    occ_i = amp_mask.shape[0]
    occ_j = pairs // occ_i

    c_own = row_id * n_col + col_id
    amp_col = lax.dynamic_slice_in_dim(amp_mask, c_own, 1, axis=1).astype(jnp.float32)
    i_local = occ_i // n_row
    amp_screened = amplitudes.reshape(occ_i, occ_j, k_local) * amp_col[:, :, None]
    amp_t = amp_screened.reshape(n_row, i_local, occ_j, k_local).transpose(3, 0, 2, 1)
    amp_t = with_layout_constraint(amp_t.reshape(k_local, pairs), Layout((0, 1)))

    c_rows = virt // n_row
    a_cols = virt // n_col
    n_local = a_cols * virt
    mask_local = lax.dynamic_slice(
        integral_mask, (row_id * c_rows, col_id * a_cols), (c_rows, a_cols)
    ).astype(jnp.float32)
    mask_wide = jnp.repeat(mask_local, virt, axis=1)
    ints = integrals.reshape(n_zy, n_core, k_local, n_local)
    masks = mask_wide.reshape(n_zy, n_core, 1, n_local)
    ints_c0 = ints[:, 0] * masks[:, 0]
    ints_c1 = ints[:, 1] * masks[:, 1]

    own = lax.all_gather(amp_t, PLANE, axis=0, tiled=True)
    own = with_layout_constraint(own, Layout((0, 1)))
    swap = [(0, 1), (1, 0)]
    first = core_id == 0
    ints_own = jnp.where(first, ints_c0, ints_c1)
    ints_other = jnp.where(first, ints_c1, ints_c0)
    ints_own, ints_other = lax.optimization_barrier((ints_own, ints_other))
    ints_lent = lax.ppermute(ints_other, "core", swap)
    own = own.reshape(n_zy, k_local, pairs)
    dims = (((0, 1), (0, 1)), ((), ()))
    lent_part = lax.dot_general(own, ints_lent, dims, precision=lax.Precision.HIGH)
    returned = lax.ppermute(lent_part, "core", swap)
    partial = lax.dot_general(own, ints_own, dims, precision=lax.Precision.HIGH) + returned

    buf = partial.reshape(n_row * occ_j, i_local, a_cols, virt)
    recv = lax.all_to_all(buf, ("row",) + COL, split_axis=0, concat_axis=0, tiled=True)
    summed = recv.reshape(n_row, n_col, i_local, a_cols, virt).sum(axis=0)
    block = summed.transpose(1, 0, 2, 3).reshape(i_local, 1, n_col * a_cols, virt)
    return block + jnp.einsum("ac,ijcb->ijab", vv_coupling, block, precision=lax.Precision.HIGHEST)


def solution(mesh):
    n_row, n_col = mesh.devices.shape
    n_side = int(round((n_col // 2) ** 0.5))
    mesh3 = Mesh(mesh.devices.reshape(n_row, n_side, n_col // 2 // n_side, 2), ("row",) + COL)
    in_specs = (P(None, ("row",) + COL), P("row", COL), P(), P(), P())
    out_specs = P("row", COL, None, None)

    return jax.shard_map(body, mesh=mesh3, in_specs=in_specs, out_specs=out_specs, check_vma=False)
```

```python
import jax
import jax.numpy as jnp
from jax import lax
from jax.experimental.layout import Layout, with_layout_constraint
from jax.sharding import Mesh

from jax.sharding import PartitionSpec as P

PLANE = ("z", "y")
COL = PLANE + ("core",)


def body(amplitudes, integrals, vv_coupling, amp_mask, integral_mask):
    n_row = lax.axis_size("row")
    n_zy = lax.axis_size(PLANE)
    n_core = lax.axis_size("core")
    n_col = n_zy * n_core
    row_id = lax.axis_index("row")
    core_id = lax.axis_index("core")
    col_id = lax.axis_index(PLANE) * n_core + core_id
    virt = vv_coupling.shape[0]
    pairs, k_local = amplitudes.shape
    occ_i = amp_mask.shape[0]
    occ_j = pairs // occ_i

    c_own = row_id * n_col + col_id
    amp_col = lax.dynamic_slice_in_dim(amp_mask, c_own, 1, axis=1).astype(jnp.float32)
    i_local = occ_i // n_row
    amp_screened = amplitudes.reshape(occ_i, occ_j, k_local) * amp_col[:, :, None]
    amp_t = amp_screened.reshape(n_row, i_local, occ_j, k_local).transpose(3, 2, 0, 1)
    amp_t = with_layout_constraint(amp_t.reshape(k_local, pairs), Layout((0, 1)))

    c_rows = virt // n_row
    a_cols = virt // n_col
    n_local = a_cols * virt
    mask_local = lax.dynamic_slice(
        integral_mask, (row_id * c_rows, col_id * a_cols), (c_rows, a_cols)
    ).astype(jnp.float32)
    mask_wide = jnp.repeat(mask_local, virt, axis=1)
    ints = integrals.reshape(n_zy, n_core, k_local, n_local)
    masks = mask_wide.reshape(n_zy, n_core, 1, n_local)
    ints_c0 = ints[:, 0] * masks[:, 0]
    ints_c1 = ints[:, 1] * masks[:, 1]

    own = lax.all_gather(amp_t, PLANE, axis=0, tiled=True)
    own = with_layout_constraint(own, Layout((0, 1)))
    swap = [(0, 1), (1, 0)]
    first = core_id == 0
    ints_own = jnp.where(first, ints_c0, ints_c1)
    ints_other = jnp.where(first, ints_c1, ints_c0)
    ints_own, ints_other = lax.optimization_barrier((ints_own, ints_other))
    ints_lent = lax.ppermute(ints_other, "core", swap)
    own = own.reshape(n_zy, k_local, pairs)
    dims = (((0, 1), (0, 1)), ((), ()))
    lent_part = lax.dot_general(own, ints_lent, dims, precision=lax.Precision.HIGH)
    returned = lax.ppermute(lent_part, "core", swap)
    partial = lax.dot_general(own, ints_own, dims, precision=lax.Precision.HIGH) + returned

    buf = partial.reshape(occ_j * n_row, i_local, a_cols, virt)
    recv = lax.all_to_all(buf, COL + ("row",), split_axis=0, concat_axis=0, tiled=True)
    summed = recv.reshape(n_col, n_row, i_local, a_cols, virt).sum(axis=1)
    block = summed.transpose(1, 0, 2, 3).reshape(i_local, 1, n_col * a_cols, virt)
    return block + jnp.einsum("ac,ijcb->ijab", vv_coupling, block, precision=lax.Precision.HIGHEST)


def solution(mesh):
    n_row, n_col = mesh.devices.shape
    n_side = int(round((n_col // 2) ** 0.5))
    mesh3 = Mesh(mesh.devices.reshape(n_row, n_side, n_col // 2 // n_side, 2), ("row",) + COL)
    in_specs = (P(None, ("row",) + COL), P("row", COL), P(), P(), P())
    out_specs = P("row", COL, None, None)

    return jax.shard_map(body, mesh=mesh3, in_specs=in_specs, out_specs=out_specs, check_vma=False)
```

```python
import jax
import jax.numpy as jnp
from jax import lax
from jax.experimental.layout import Layout, with_layout_constraint
from jax.sharding import Mesh

from jax.sharding import PartitionSpec as P

PLANE = ("z", "y")
COL = PLANE + ("core",)


def body(amplitudes, integrals, vv_coupling, amp_mask, integral_mask):
    n_row = lax.axis_size("row")
    n_zy = lax.axis_size(PLANE)
    n_core = lax.axis_size("core")
    n_col = n_zy * n_core
    row_id = lax.axis_index("row")
    core_id = lax.axis_index("core")
    col_id = lax.axis_index(PLANE) * n_core + core_id
    virt = vv_coupling.shape[0]
    pairs, k_local = amplitudes.shape
    occ_i = amp_mask.shape[0]
    occ_j = pairs // occ_i

    c_own = row_id * n_col + col_id
    amp_col = lax.dynamic_slice_in_dim(amp_mask, c_own, 1, axis=1).astype(jnp.float32)
    i_local = occ_i // n_row
    amp_screened = amplitudes.reshape(occ_i, occ_j, k_local) * amp_col[:, :, None]
    amp_t = amp_screened.reshape(n_row, i_local, occ_j, k_local).transpose(3, 0, 2, 1)
    amp_t = with_layout_constraint(amp_t.reshape(k_local, pairs), Layout((0, 1)))

    c_rows = virt // n_row
    a_cols = virt // n_col
    n_local = a_cols * virt
    mask_local = lax.dynamic_slice(
        integral_mask, (row_id * c_rows, col_id * a_cols), (c_rows, a_cols)
    ).astype(jnp.float32)
    mask_wide = jnp.repeat(mask_local, virt, axis=1)
    ints = integrals.reshape(n_zy, n_core, k_local, n_local)
    masks = mask_wide.reshape(n_zy, n_core, 1, n_local)
    ints_c0 = ints[:, 0] * masks[:, 0]
    ints_c1 = ints[:, 1] * masks[:, 1]

    own = lax.all_gather(amp_t, PLANE, axis=0, tiled=True)
    own = with_layout_constraint(own, Layout((0, 1)))
    swap = [(0, 1), (1, 0)]
    first = core_id == 0
    ints_own = jnp.where(first, ints_c0, ints_c1)
    ints_other = jnp.where(first, ints_c1, ints_c0)
    ints_own, ints_other = lax.optimization_barrier((ints_own, ints_other))
    ints_lent = lax.ppermute(ints_other, "core", swap)
    own = own.reshape(n_zy, k_local, pairs)
    dims = (((0, 1), (0, 1)), ((), ()))
    lent_part = lax.dot_general(own, ints_lent, dims, precision=lax.Precision.HIGH)
    returned = lax.ppermute(lent_part, "core", swap)
    partial = lax.dot_general(own, ints_own, dims, precision=lax.Precision.HIGH) + returned

    buf = partial.reshape(n_row * occ_j, i_local, a_cols, virt)
    recv = lax.all_to_all(buf, ("row",) + COL, split_axis=0, concat_axis=0, tiled=True)
    summed = recv.reshape(n_row, n_col, i_local, a_cols, virt).sum(axis=0)
    block = summed.transpose(1, 0, 2, 3).reshape(i_local, 1, n_col * a_cols, virt)
    row_major = Layout((0, 1, 2, 3))
    block = with_layout_constraint(block, row_major)
    out = block + jnp.einsum("ac,ijcb->ijab", vv_coupling, block, precision=lax.Precision.HIGHEST)
    return with_layout_constraint(out, row_major)


def solution(mesh):
    n_row, n_col = mesh.devices.shape
    n_side = int(round((n_col // 2) ** 0.5))
    mesh3 = Mesh(mesh.devices.reshape(n_row, n_side, n_col // 2 // n_side, 2), ("row",) + COL)
    in_specs = (P(None, ("row",) + COL), P("row", COL), P(), P(), P())
    out_specs = P("row", COL, None, None)

    return jax.shard_map(body, mesh=mesh3, in_specs=in_specs, out_specs=out_specs, check_vma=False)
```
